32 devices in a mesh: band: 2 (over x), grid: 16 (over z, y, core).
Axes of the slice: x: 2, y: 2, z: 4, core: 2. Of those that a mesh axis runs over, the one named last changes fastest.
Arguments:
- start_block: float32 [64, 128, 4, 128], P('band', 'grid'), may hold values from -6 to 6
- previous_block: float32 [64, 128, 4, 128], P('band', 'grid'), may hold values from -6 to 6
- previous_coupling: float32 [64, 64], replicated, may hold values from -0.75 to 0.75
- potential: float32 [128, 4, 128], P('grid'), may hold values from -2 to 2
- atom_cells: int32 [128, 128], P('grid'), may hold values from 0 to 7167, as said below
- atom_proj: float32 [128, 4, 128], P('grid'), may hold values from -1.08 to 1.08
- atom_strength: float32 [128, 4], P('grid'), may hold values from 0.5 to 4
- atom_count: int32 [16], P('grid'), may hold values from 1 to 8, as said below
Outputs:
- a_blocks: float32 [2, 64, 64], P(None, None, 'band')
- b_blocks: float32 [2, 64, 64], P(None, None, 'band')
- final_block: float32 [64, 128, 4, 128], P('band', 'grid')
The draws below stay inside these ranges and needn't reach their ends.
Inputs may be any that keep to these rules, and one draw needn't show every extreme that they name: `atom_cells`: row a lists 128 distinct cells of atom a's sphere as row-major indices over (14) planes x 4 x 128, counted from the first plane of the slab that holds row a; indices of 4096 or more lie in the first 6 planes of the next slab; on the last slab every index is below 4096. `atom_count`: slots at or past a slab's count are not atoms.
All inputs are finite; a program needn't handle non-finite values.
Results may differ from the reference program's by a relative error of at most 0.0003.
Values sent between devices are 32-bit elements; how exact they have to be, the bound alone decides.
A program may use at most 64 MiB of HBM per device.

```python
import math
import jax
import jax.numpy as jnp
from jax import lax

NB = 64
CX = 8
NY = 4
NZ = 128
ATOM_DEV = 8
PTS = 128
NPROJ = 4
STEPS = 2
NX = 128
NATOM = 128
N_GRID = 16


def draw_atom_cells(key, part):
    key_x, key_y, key_z = jax.random.split(key, 3)
    atom_rows = jnp.arange(NATOM, dtype=jnp.int32)
    last_dev = atom_rows // ATOM_DEV == N_GRID - 1
    top_x = jnp.where(last_dev, CX - 4, CX + 2)
    corner_x = jax.random.randint(key_x, (NATOM,), 0, top_x + 1)
    corner_y = jax.random.randint(key_y, (NATOM,), 0, NY - 3)
    corner_z = jax.random.randint(key_z, (NATOM,), 0, NZ - 7)
    corner_x = corner_x.at[0].set(CX + 2).at[1].set(0)
    corner_y = corner_y.at[0].set(NY - 4).at[1].set(0)
    corner_z = corner_z.at[0].set(NZ - 8).at[1].set(0)
    points = jnp.arange(PTS, dtype=jnp.int32)
    offset_x = points // 32
    offset_y = points // 8 % 4
    offset_z = points % 8
    cell_index = ((corner_x[:, None] + offset_x[None]) * NY + corner_y[:, None] + offset_y[None]) * NZ + corner_z[:, None] + offset_z[None]
    return cell_index.astype(jnp.int32)


def draw_atom_count(key, part):
    key_a, key_b = jax.random.split(key, 2)
    counts = jax.random.randint(key_a, (N_GRID,), 1, ATOM_DEV + 1)
    fullest = jax.random.randint(key_b, (), 0, N_GRID)
    return jnp.where(jnp.arange(N_GRID, dtype=jnp.int32) == fullest, ATOM_DEV, counts).astype(jnp.int32)


def block_levels(rng, shape, pieces, low, top_value):
    loudness, own = 1.0, jax.random.fold_in(rng, 6)
    for dim, parts in pieces:
        steps = jnp.exp(jax.random.uniform(jax.random.fold_in(own, dim), (parts,), jnp.float32, low / len(pieces), top_value / len(pieces)))
        loudness = loudness * jnp.repeat(steps, shape[dim] // parts).reshape([-1 if axis == dim else 1 for axis in range(len(shape))])
    return loudness


def bell_draw(own_key, dims, width, limit, shards=(), held_as=jnp.bfloat16):
    loudness = block_levels(own_key, dims, shards, -0.22, 0.18) if shards else 1.0
    drawn = jax.random.normal(own_key, dims, jnp.float32) * width * loudness
    return jnp.minimum(jnp.maximum(drawn, -limit), limit).astype(held_as)


def setup_inputs(seed: int = 0) -> dict:
    keys = jax.random.split(jax.random.key(seed), 9)
    return {
        "start_block": bell_draw(keys[0], (NB, NX, NY, NZ), 1.0, 6.0, ((0, 2), (1, 16)), jnp.float32),
        "previous_block": bell_draw(keys[1], (NB, NX, NY, NZ), 1.0, 6.0, ((0, 2), (1, 16)), jnp.float32),
        "previous_coupling": bell_draw(keys[2], (NB, NB), NB ** -0.5, 0.75, (), jnp.float32),
        "potential": jnp.clip(jax.random.uniform(keys[3], (NX, NY, NZ), jnp.float32, -2.0, 2.0) * block_levels(keys[3], (NX, NY, NZ), ((0, 16),), -0.4, 0.0), -2.0, 2.0),
        "atom_cells": draw_atom_cells(jax.random.fold_in(keys[8], 71), 0),
        "atom_proj": bell_draw(keys[5], (NATOM, NPROJ, PTS), 0.18, 1.08, ((0, 16),), jnp.float32),
        "atom_strength": jnp.clip(jnp.exp(math.log(4.0) - 2.0794415 * jax.random.uniform(keys[6], (NATOM, NPROJ), jnp.float32) ** block_levels(keys[6], (NATOM, NPROJ), ((0, 16),), -0.2, 0.2)), 0.5, 4.0),
        "atom_count": draw_atom_count(jax.random.fold_in(keys[8], 71), 0),
    }


HIGHEST = lax.Precision.HIGHEST
STENCIL_WEIGHTS = (-5369.0 / 1800.0, 12.0 / 7.0, -15.0 / 56.0, 10.0 / 189.0, -1.0 / 112.0, 2.0 / 1925.0, -1.0 / 16632.0)

def kinetic(field_in):
    sizes_x, sizes_y, sizes_z = (field_in.shape[1], field_in.shape[2], field_in.shape[3])
    padded = jnp.pad(field_in, ((0, 0), (6, 6), (6, 6), (6, 6)))
    laplace = 3.0 * STENCIL_WEIGHTS[0] * field_in
    for k in range(1, 7):
        laplace = laplace + STENCIL_WEIGHTS[k] * (padded[:, 6 + k:6 + k + sizes_x, 6:6 + sizes_y, 6:6 + sizes_z] + padded[:, 6 - k:6 - k + sizes_x, 6:6 + sizes_y, 6:6 + sizes_z])
        laplace = laplace + STENCIL_WEIGHTS[k] * (padded[:, 6:6 + sizes_x, 6 + k:6 + k + sizes_y, 6:6 + sizes_z] + padded[:, 6:6 + sizes_x, 6 - k:6 - k + sizes_y, 6:6 + sizes_z])
        laplace = laplace + STENCIL_WEIGHTS[k] * (padded[:, 6:6 + sizes_x, 6:6 + sizes_y, 6 + k:6 + k + sizes_z] + padded[:, 6:6 + sizes_x, 6:6 + sizes_y, 6 - k:6 - k + sizes_z])
    return -0.5 * laplace

def projector_term(flattened, atom_cells, atom_proj, atom_strength, atom_count):
    atom_slots = atom_cells.shape[0]
    atom_rows = jnp.arange(atom_slots, dtype=jnp.int32)
    home_dev = atom_rows // ATOM_DEV
    global_cells = (home_dev * (CX * NY * NZ))[:, None] + atom_cells
    live_mask = (atom_rows % ATOM_DEV < atom_count[home_dev]).astype(jnp.float32)
    cell_list = global_cells.reshape(-1)
    picked = flattened[:, cell_list].reshape(NB, atom_slots, PTS)
    coefficient = jnp.einsum('bap,ajp->baj', picked, atom_proj, precision=HIGHEST)
    scaled = coefficient * (atom_strength * live_mask[:, None])[None]
    spread = jnp.einsum('baj,ajp->bap', scaled, atom_proj, precision=HIGHEST)
    return jnp.zeros_like(flattened).at[:, cell_list].add(spread.reshape(NB, -1))

def apply_operator(flattened, potential, atom_cells, atom_proj, atom_strength, atom_count):
    kinetic_part = kinetic(flattened.reshape(NB, NX, NY, NZ)).reshape(NB, -1)
    return kinetic_part + potential.reshape(1, -1) * flattened + projector_term(flattened, atom_cells, atom_proj, atom_strength, atom_count)

def orthonormal(block):
    cell_total = NX * NY * NZ
    gram = jnp.dot(block, block.T, precision=HIGHEST) / cell_total
    factor = jnp.linalg.cholesky(gram)
    identity = jnp.eye(NB, dtype=gram.dtype)
    inverse = jax.scipy.linalg.solve_triangular(factor, identity, lower=True)
    return (jnp.dot(inverse, block, precision=HIGHEST), factor.T)

def reference(start_block, previous_block, previous_coupling, potential, atom_cells, atom_proj, atom_strength, atom_count):
    cell_total = NX * NY * NZ
    current, unused = orthonormal(start_block.reshape(NB, -1))
    previous = previous_block.reshape(NB, -1)
    coupling = previous_coupling
    a_list = []
    b_list = []
    for iteration in range(STEPS):
        applied = apply_operator(current, potential, atom_cells, atom_proj, atom_strength, atom_count)
        correlation = jnp.dot(current, applied.T, precision=HIGHEST) / cell_total
        residual_block = applied - jnp.dot(correlation.T, current, precision=HIGHEST) - jnp.dot(coupling, previous, precision=HIGHEST)
        following, coupling_new = orthonormal(residual_block)
        a_list.append(correlation)
        b_list.append(coupling_new)
        previous = current
        current = following
        coupling = coupling_new
    return (jnp.stack(a_list), jnp.stack(b_list), current.reshape(NB, NX, NY, NZ))
```

```python
import functools

import jax
import jax.numpy as jnp
from jax import lax
from jax.experimental import pallas as pl
from jax.experimental.pallas import tpu as pltpu
from jax.sharding import PartitionSpec as P

NB = 64
STEPS = 2
HALO = 6
MESH = pl.DeviceIdType.MESH

HIGHEST = lax.Precision.HIGHEST
STENCIL_WEIGHTS = (
    -5369.0 / 1800.0,
    12.0 / 7.0,
    -15.0 / 56.0,
    10.0 / 189.0,
    -1.0 / 112.0,
    2.0 / 1925.0,
    -1.0 / 16632.0,
)
HOP = tuple(-0.5 * w for w in STENCIL_WEIGHTS)
SHIFT = 3.0 * HOP[0]
BLOCKS = 5
PAIRS = [(i, j) for i in range(BLOCKS) for j in range(i, BLOCKS)]
F32 = jnp.float32
BF16 = jnp.bfloat16


def split(x):
    high = x.astype(BF16)
    return high, (x - high.astype(F32)).astype(BF16)


def dot_nt(a, b):
    return lax.dot_general(a, b, (((1,), (1,)), ((), ())), preferred_element_type=F32)


def dot_nn(a, b):
    return lax.dot_general(a, b, (((1,), (0,)), ((), ())), preferred_element_type=F32)


def krylov_kernel(
    nb, ng, planes, wy, slots, nproj, owners,
    x_ref, p_ref, pot_ref, cells_ref, proj_ref, scale_ref,
    s_ref, g_ref,
    ext, fin, dens_h, dens_l, prev_h, prev_l, prev_cells, prev_proj,
    csend, cprev, gpart, grecv, gown,
    halo_send, halo_recv, meta_send, meta_recv, c_send, c_recv,
    band_send, band_recv, rs_send, rs_recv, ag_send, ag_recv,
):
    ndev = nb * ng
    states = x_ref.shape[0] // (planes * wy)
    lines = planes * wy
    edge = HALO * wy
    part = lines // nb
    rows = slots * nproj
    wz = x_ref.shape[1]
    span = wy * wz
    band = lax.axis_index("band")
    grid = lax.axis_index("grid")
    me = band * ng + grid
    has_prev = grid > 0
    has_next = grid < ng - 1
    before = (band, jnp.maximum(grid - 1, 0))
    behind = (band, jnp.minimum(grid + 1, ng - 1))

    barrier = pltpu.get_barrier_semaphore()

    def greet(d, carry):
        t = lax.rem(me + d, ndev)
        pl.semaphore_signal(barrier, inc=1, device_id=(t // ng, lax.rem(t, ng)), device_id_type=MESH)
        return carry

    lax.fori_loop(1, ndev, greet, 0)

    def load(i, carry):
        ext[0, edge + i] = x_ref[pl.ds(i, states, stride=lines), :]
        ext[1, edge + i] = p_ref[pl.ds(i, states, stride=lines), :]
        return carry

    lax.fori_loop(0, lines, load, 0)

    @pl.when(jnp.logical_not(has_prev))
    def _():
        for b in range(3):
            ext[b, 0:edge] = jnp.zeros((edge, states, wz), F32)
            cprev[b] = jnp.zeros_like(cprev[b])
        prev_cells[...] = jnp.zeros_like(prev_cells)
        prev_proj[...] = jnp.zeros_like(prev_proj)

    @pl.when(jnp.logical_not(has_next))
    def _():
        for b in range(3):
            ext[b, edge + lines :] = jnp.zeros((edge, states, wz), F32)

    def dense(cells, proj, first, count, out_h, out_l):
        per = 8 // nproj
        line_iota = lax.broadcasted_iota(jnp.int32, (count, 8, per * wz), 0) + first
        lane_iota = lax.broadcasted_iota(jnp.int32, (wz, per * wz), 0)
        row_iota = lax.broadcasted_iota(jnp.int32, (8, wz), 0)
        for q in range(slots // per):
            values = proj[8 * q : 8 * q + 8, :]
            spread = jnp.concatenate(
                [jnp.where(row_iota // nproj == u, values, 0.0) for u in range(per)], axis=1
            )
            where = jnp.concatenate(
                [cells[per * q + u : per * q + u + 1, :] for u in range(per)], axis=1
            )
            hot = jnp.where(lane_iota == where % wz, 1.0, 0.0).astype(BF16)
            hit = line_iota == (where // wz)[None]
            for source, out in zip(split(spread), (out_h, out_l)):
                left = jnp.where(hit, source.astype(F32)[None], 0.0)
                left = left.reshape(count * 8, per * wz).astype(BF16)
                made = dot_nt(left, hot).reshape(count, 8, wz)
                out[0:count, 8 * q : 8 * q + 8, :] = made

    dense(cells_ref, proj_ref, 0, lines + edge, dens_h, dens_l)

    pl.semaphore_wait(barrier, ndev - 1)

    def up_copy(b):
        return pltpu.make_async_remote_copy(
            ext.at[b, pl.ds(lines, edge)], ext.at[b, pl.ds(0, edge)],
            halo_send.at[2 * b], halo_recv.at[2 * b], behind, MESH)

    def down_copy(b):
        return pltpu.make_async_remote_copy(
            ext.at[b, pl.ds(edge, edge)], ext.at[b, pl.ds(edge + lines, edge)],
            halo_send.at[2 * b + 1], halo_recv.at[2 * b + 1], before, MESH)

    def meta_copies():
        return (
            pltpu.make_async_remote_copy(
                cells_ref, prev_cells, meta_send.at[0], meta_recv.at[0], behind, MESH),
            pltpu.make_async_remote_copy(
                proj_ref, prev_proj, meta_send.at[1], meta_recv.at[1], behind, MESH),
        )

    def c_copy(b):
        return pltpu.make_async_remote_copy(
            csend.at[b], cprev.at[b], c_send.at[b], c_recv.at[b], behind, MESH)

    def start_halo(b):
        @pl.when(has_next)
        def _():
            up_copy(b).start()

        @pl.when(has_prev)
        def _():
            down_copy(b).start()

    def block_lines(b):
        return (ext.at[b], edge) if b < 3 else (fin.at[b - 3], 0)

    def band_copy(b, d):
        t = lax.rem(band + d, nb)
        ref, base = block_lines(b)
        return pltpu.make_async_remote_copy(
            ref.at[pl.ds(base + part * t, part)],
            s_ref.at[b, :, pl.ds(pl.multiple_of(band * states, states), states), :],
            band_send.at[b, d - 1], band_recv.at[b, d - 1], (t, grid), MESH)

    def start_band(b):
        for d in range(1, nb):
            band_copy(b, d).start()
        ref, base = block_lines(b)
        s_ref[b, :, pl.ds(pl.multiple_of(band * states, states), states), :] = ref[
            pl.ds(base + part * band, part)]

    @pl.when(has_next)
    def _():
        for copy in meta_copies():
            copy.start()

    start_halo(0)
    start_band(0)
    start_halo(1)
    start_band(1)

    @pl.when(has_prev)
    def _():
        for copy in meta_copies():
            copy.wait_recv()

    prev_h[edge:lines] = jnp.zeros((lines - edge, rows, wz), F32)
    prev_l[edge:lines] = jnp.zeros((lines - edge, rows, wz), F32)
    dense(prev_cells, prev_proj, lines, edge, prev_h, prev_l)

    lane = lax.broadcasted_iota(jnp.int32, (1, wz), 1)
    ups = [jnp.where(lane >= k, HOP[k], 0.0).astype(F32) for k in range(1, 7)]
    downs = [jnp.where(lane < wz - k, HOP[k], 0.0).astype(F32) for k in range(1, 7)]

    def wide(ref, first):
        return jnp.concatenate([ref[first + y] for y in range(wy)], axis=1)

    def apply(b, store):
        @pl.when(has_prev)
        def _():
            up_copy(b).wait_recv()

        @pl.when(has_next)
        def _():
            down_copy(b).wait_recv()

        def project(p, carry):
            value = jnp.concatenate([ext[b, edge + wy * p + y] for y in range(wy)], axis=1)
            high, low = split(value)
            d_h = wide(dens_h, wy * p).astype(BF16)
            d_l = wide(dens_l, wy * p).astype(BF16)
            both = dot_nt(high, d_h) + dot_nt(low, d_h)
            return carry + both + dot_nt(high, d_l)

        coefficient = lax.fori_loop(
            0, planes + HALO, project, jnp.zeros((states, rows), F32), unroll=2)
        scaled = coefficient * scale_ref[...]
        csend[b, :, 0:rows] = scaled

        @pl.when(has_next)
        def _():
            c_copy(b).start()

        own_h, own_l = split(scaled)

        def plane(p, carry):
            here = edge + wy * p
            center = [ext[b, here + y] for y in range(wy)]
            d_h = wide(dens_h, wy * p).astype(BF16)
            d_l = wide(dens_l, wy * p).astype(BF16)
            term = dot_nn(own_h, d_h) + dot_nn(own_l, d_h) + dot_nn(own_h, d_l)
            for y in range(wy):
                v = center[y]
                total = pot_ref[pl.ds(wy * p + y, 1), :] * v + term[:, y * wz : (y + 1) * wz]
                for k in range(1, 7):
                    total = total + HOP[k] * (
                        ext[b, here + wy * k + y] + ext[b, here - wy * k + y])
                for other in range(wy):
                    if 0 < abs(other - y) <= 6:
                        total = total + HOP[abs(other - y)] * center[other]
                for k in range(1, 7):
                    total = total + ups[k - 1] * pltpu.roll(v, k, 1)
                    total = total + downs[k - 1] * pltpu.roll(v, wz - k, 1)
                store(wy * p + y, total)
            return carry

        lax.fori_loop(0, planes, plane, 0)

        @pl.when(has_prev)
        def _():
            c_copy(b).wait_recv()

        got_h, got_l = split(cprev[b, :, 0:rows])

        def outer(p, carry):
            d_h = wide(prev_h, wy * p).astype(BF16)
            d_l = wide(prev_l, wy * p).astype(BF16)
            term = dot_nn(got_h, d_h) + dot_nn(got_l, d_h) + dot_nn(got_h, d_l)
            for y in range(wy):
                store(wy * p + y, term[:, y * wz : (y + 1) * wz], True)
            return carry

        lax.fori_loop(0, HALO, outer, 0)

    def store_to(ref, base):
        def store(i, value, add=False):
            if add:
                ref[base + i] = ref[base + i] + value
            else:
                ref[base + i] = value
        return store

    apply(0, store_to(ext.at[2], edge))
    start_halo(2)
    start_band(2)
    apply(1, store_to(fin.at[0], 0))
    start_band(3)
    apply(2, store_to(fin.at[1], 0))
    start_band(4)

    for b in range(BLOCKS):
        for d in range(1, nb):
            band_copy(b, d).wait_recv()

    many = 4 if part % 4 == 0 else 1

    def gram(i, carry):
        value = jnp.concatenate(
            [
                jnp.concatenate([s_ref[b, many * i + u] for b in range(BLOCKS)], axis=0)
                for u in range(many)
            ],
            axis=1,
        )
        high, low = split(value)
        return carry + dot_nt(high, high) + dot_nt(high, low) + dot_nt(low, high)

    total = lax.fori_loop(
        0, part // many, gram, jnp.zeros((BLOCKS * NB, BLOCKS * NB), F32))
    for n, (i, j) in enumerate(PAIRS):
        gpart[NB * (n // 2) : NB * (n // 2) + NB, NB * (n % 2) : NB * (n % 2) + NB] = total[
            NB * i : NB * i + NB, NB * j : NB * j + NB]
    gpart[NB * 7 :, NB:] = jnp.zeros((NB, NB), F32)

    share = gpart.shape[0] // owners

    def piece(index):
        return pl.ds(pl.multiple_of(index * share, share), share)

    def device(t):
        return (t // ng, lax.rem(t, ng))

    def rs_copy(d):
        t = lax.rem(me + d, ndev)
        return t, pltpu.make_async_remote_copy(
            gpart.at[piece(jnp.minimum(t, owners - 1))], grecv.at[d - 1],
            rs_send.at[d - 1], rs_recv.at[d - 1], device(t), MESH)

    def ag_copy(d, source):
        t = lax.rem(me + d, ndev)
        mine = piece(jnp.minimum(source, owners - 1))
        return pltpu.make_async_remote_copy(
            gown, g_ref.at[mine], ag_send.at[d - 1], ag_recv.at[d - 1], device(t), MESH)

    def guard(cond, body):
        if owners == ndev:
            body()
        else:
            pl.when(cond)(body)

    def rs_start(d, carry):
        t, copy = rs_copy(d)
        guard(t < owners, lambda: copy.start())
        return carry

    lax.fori_loop(1, ndev, rs_start, 0)

    def own_sum():
        def add(d, acc):
            _, copy = rs_copy(d)
            copy.wait_recv()
            return acc + grecv[d - 1]

        summed = lax.fori_loop(1, ndev, add, gpart[piece(jnp.minimum(me, owners - 1)), :])
        gown[...] = summed
        g_ref[piece(jnp.minimum(me, owners - 1)), :] = summed

        def ag_start(d, carry):
            ag_copy(d, me).start()
            return carry

        lax.fori_loop(1, ndev, ag_start, 0)

    guard(me < owners, own_sum)

    def ag_wait(d, carry):
        source = lax.rem(me + ndev - d, ndev)
        guard(source < owners, lambda: ag_copy(d, source).wait_recv())
        return carry

    lax.fori_loop(1, ndev, ag_wait, 0)

    def drain(d, carry):
        t, copy = rs_copy(d)
        guard(t < owners, lambda: copy.wait_send())
        guard(me < owners, lambda: ag_copy(d, me).wait_send())
        return carry

    lax.fori_loop(1, ndev, drain, 0)

    for b in range(BLOCKS):
        for d in range(1, nb):
            band_copy(b, d).wait_send()

    @pl.when(has_next)
    def _():
        for b in range(3):
            up_copy(b).wait_send()
            c_copy(b).wait_send()
        for copy in meta_copies():
            copy.wait_send()

    @pl.when(has_prev)
    def _():
        for b in range(3):
            down_copy(b).wait_send()


def final_kernel(nb, ng, m_ref, s_ref, q_ref, mine, got, sends, recvs):
    band = lax.axis_index("band")
    grid = lax.axis_index("grid")
    part = s_ref.shape[1]
    states = NB // nb
    lines = part * nb
    barrier = pltpu.get_barrier_semaphore()
    for d in range(1, nb):
        pl.semaphore_signal(
            barrier, inc=1, device_id=(lax.rem(band + d, nb), grid), device_id_type=MESH)
    high, low = split(m_ref[...])

    def combine(i, carry):
        value = jnp.concatenate([s_ref[b, i] for b in range(BLOCKS)], axis=0)
        v_h, v_l = split(value)
        made = dot_nn(high, v_h) + dot_nn(low, v_h) + dot_nn(high, v_l)
        for t in range(nb):
            mine[t, i] = made[t * states : (t + 1) * states]
        return carry

    lax.fori_loop(0, part, combine, 0, unroll=2)
    pl.semaphore_wait(barrier, nb - 1)

    def copy(d):
        t = lax.rem(band + d, nb)
        return pltpu.make_async_remote_copy(
            mine.at[t], got.at[band], sends.at[d - 1], recvs.at[d - 1], (t, grid), MESH)

    for d in range(1, nb):
        copy(d).start()

    def put(source, ref):
        def line(i, carry):
            q_ref[pl.ds(source * part + i, states, stride=lines), :] = ref[i]
            return carry

        lax.fori_loop(0, part, line, 0)

    put(band, mine.at[band])
    for d in range(1, nb):
        copy(d).wait_recv()
        source = lax.rem(band + nb - d, nb)
        put(source, got.at[source])
    for d in range(1, nb):
        copy(d).wait_send()


def factor_of(gram):
    factor = jnp.linalg.cholesky(gram)
    identity = jnp.eye(gram.shape[0], dtype=F32)
    inverse = jax.scipy.linalg.solve_triangular(factor, identity, lower=True)
    return (factor, inverse)


def mm(*factors):
    value = factors[0]
    for other in factors[1:]:
        value = jnp.dot(value, other, precision=HIGHEST)
    return value


def shards(
    start_block,
    previous_block,
    previous_coupling,
    potential,
    atom_cells,
    atom_proj,
    atom_strength,
    atom_count,
):
    states, planes, wy, wz = start_block.shape
    slots, nproj, points = atom_proj.shape
    nb, ng = lax.axis_size("band"), lax.axis_size("grid")
    ndev = nb * ng
    lines = planes * wy
    edge = HALO * wy
    part = lines // nb
    rows = slots * nproj
    cell_total = lines * ng * wz
    owners = min(ndev, 64)
    live = (jnp.arange(slots, dtype=jnp.int32) < atom_count[0]).astype(F32)
    scale = (atom_strength * live[:, None]).reshape(1, rows)
    dma = pltpu.SemaphoreType.DMA
    vmem = pl.BlockSpec(memory_space=pltpu.VMEM)
    grows = NB * 8
    basis, packed = pl.pallas_call(
        functools.partial(krylov_kernel, nb, ng, planes, wy, slots, nproj, owners),
        out_shape=(
            jax.ShapeDtypeStruct((BLOCKS, part, NB, wz), F32),
            jax.ShapeDtypeStruct((grows, 2 * NB), F32),
        ),
        in_specs=[vmem] * 6,
        out_specs=(vmem, vmem),
        scratch_shapes=[
            pltpu.VMEM((3, lines + 2 * edge, states, wz), F32),
            pltpu.VMEM((2, lines, states, wz), F32),
            pltpu.VMEM((lines + edge, rows, wz), F32),
            pltpu.VMEM((lines + edge, rows, wz), F32),
            pltpu.VMEM((lines, rows, wz), F32),
            pltpu.VMEM((lines, rows, wz), F32),
            pltpu.VMEM((slots, points), jnp.int32),
            pltpu.VMEM((rows, points), F32),
            pltpu.VMEM((3, states, 128), F32),
            pltpu.VMEM((3, states, 128), F32),
            pltpu.VMEM((grows, 2 * NB), F32),
            pltpu.VMEM((ndev - 1, grows // owners, 2 * NB), F32),
            pltpu.VMEM((grows // owners, 2 * NB), F32),
            dma((6,)), dma((6,)), dma((2,)), dma((2,)), dma((3,)), dma((3,)),
            dma((BLOCKS, nb - 1)), dma((BLOCKS, nb - 1)),
            dma((ndev - 1,)), dma((ndev - 1,)), dma((ndev - 1,)), dma((ndev - 1,)),
        ],
        compiler_params=pltpu.CompilerParams(
            collective_id=0, has_side_effects=True, vmem_limit_bytes=48 * 2**20),
    )(
        start_block.reshape(states * lines, wz),
        previous_block.reshape(states * lines, wz),
        potential.reshape(lines, wz),
        atom_cells,
        atom_proj.reshape(rows, points),
        scale,
    )
    packed = packed / cell_total
    g = {}
    for n, (i, j) in enumerate(PAIRS):
        block = packed[NB * (n // 2) : NB * (n // 2) + NB, NB * (n % 2) : NB * (n % 2) + NB]
        g[i, j] = block
        if i != j:
            g[j, i] = block.T
    whole = jnp.concatenate(
        [jnp.concatenate([g[i, j] for j in range(BLOCKS)], axis=1) for i in range(BLOCKS)], axis=0)
    zero = jnp.zeros((NB, NB), F32)
    factor, inverse = factor_of(g[0, 0])
    row = lambda *parts: jnp.concatenate(parts, axis=1)
    identity = jnp.eye(NB, dtype=F32)
    a_shifted = mm(inverse, g[0, 2], inverse.T)
    w0 = row(-mm(a_shifted.T, inverse), -previous_coupling, inverse, zero, zero)
    factor, inverse1 = factor_of(mm(w0, whole, w0.T))
    q0 = row(inverse, zero, zero, zero, zero)
    q1 = mm(inverse1, w0)
    hq1 = row(zero, zero, q1[:, :NB], q1[:, NB : 2 * NB], q1[:, 2 * NB : 3 * NB])
    a1_shifted = mm(q1, whole, hq1.T)
    coupling = factor.T
    w1 = hq1 - mm(a1_shifted.T, q1) - mm(coupling, q0)
    factor1, inverse2 = factor_of(mm(w1, whole, w1.T))
    q2 = mm(inverse2, w1)
    final = pl.pallas_call(
        functools.partial(final_kernel, nb, ng),
        out_shape=jax.ShapeDtypeStruct((states * lines, wz), F32),
        in_specs=[vmem] * 2,
        out_specs=vmem,
        scratch_shapes=[
            pltpu.VMEM((nb, part, states, wz), F32),
            pltpu.VMEM((nb, part, states, wz), F32),
            dma((nb - 1,)), dma((nb - 1,)),
        ],
        compiler_params=pltpu.CompilerParams(
            collective_id=1, has_side_effects=True, vmem_limit_bytes=32 * 2**20),
    )(q2, basis)
    offset = lax.axis_index("band") * states
    pick = lambda m: lax.dynamic_slice_in_dim(m, offset, states, 1)
    a_list = [pick(a_shifted + SHIFT * identity), pick(a1_shifted + SHIFT * identity)]
    b_list = [pick(factor.T), pick(factor1.T)]
    return (jnp.stack(a_list), jnp.stack(b_list), final.reshape(start_block.shape))


def solution(mesh):
    in_specs = (
        P("band", "grid", None, None),
        P("band", "grid", None, None),
        P(),
        P("grid", None, None),
        P("grid", None),
        P("grid", None, None),
        P("grid", None),
        P("grid"),
    )
    out_specs = (P(None, None, "band"), P(None, None, "band"), P("band", "grid", None, None))
    return jax.shard_map(shards, mesh=mesh, in_specs=in_specs, out_specs=out_specs, check_vma=False)
```

```python
import functools

import jax
import jax.numpy as jnp
from jax import lax
from jax.experimental import pallas as pl
from jax.experimental.pallas import tpu as pltpu
from jax.sharding import PartitionSpec as P

NB = 64
STEPS = 2
HALO = 6
MESH = pl.DeviceIdType.MESH

HIGHEST = lax.Precision.HIGHEST
STENCIL_WEIGHTS = (
    -5369.0 / 1800.0,
    12.0 / 7.0,
    -15.0 / 56.0,
    10.0 / 189.0,
    -1.0 / 112.0,
    2.0 / 1925.0,
    -1.0 / 16632.0,
)
HOP = tuple(-0.5 * w for w in STENCIL_WEIGHTS)
SHIFT = 3.0 * HOP[0]
BLOCKS = 5
PAIRS = [(i, j) for i in range(BLOCKS) for j in range(i, BLOCKS)]
F32 = jnp.float32
BF16 = jnp.bfloat16


def split(x):
    high = x.astype(BF16)
    return high, (x - high.astype(F32)).astype(BF16)


def dot_nt(a, b):
    return lax.dot_general(a, b, (((1,), (1,)), ((), ())), preferred_element_type=F32)


def dot_nn(a, b):
    return lax.dot_general(a, b, (((1,), (0,)), ((), ())), preferred_element_type=F32)


def krylov_kernel(
    nb, ng, planes, wy, slots, nproj, owners,
    x_hbm, p_hbm, pot_hbm, cells_hbm, proj_hbm, scale_hbm, prior_hbm,
    small_ref, q_ref,
    x_ref, p_ref, pot_ref, cells_ref, proj_ref, scale_ref, prior_ref, in_sems,
    s_ref, g_ref, whole, co, mat, mine, got, out_send, out_recv,
    ext, fin, dens_h, dens_l, prev_h, prev_l, prev_cells, prev_proj,
    csend, cprev, gpart, grecv, gown,
    halo_send, halo_recv, meta_send, meta_recv, c_send, c_recv,
    band_send, band_recv, rs_send, rs_recv, ag_send, ag_recv,
):
    ndev = nb * ng
    states = x_ref.shape[0] // (planes * wy)
    lines = planes * wy
    edge = HALO * wy
    part = lines // nb
    rows = slots * nproj
    wz = x_ref.shape[1]
    span = wy * wz
    band = lax.axis_index("band")
    grid = lax.axis_index("grid")
    me = band * ng + grid
    has_prev = grid > 0
    has_next = grid < ng - 1
    before = (band, jnp.maximum(grid - 1, 0))
    behind = (band, jnp.minimum(grid + 1, ng - 1))

    barrier = pltpu.get_barrier_semaphore()

    def greet(d, carry):
        t = lax.rem(me + d, ndev)
        pl.semaphore_signal(barrier, inc=1, device_id=(t // ng, lax.rem(t, ng)), device_id_type=MESH)
        return carry

    loads = [
        pltpu.make_async_copy(source, target, in_sems.at[n])
        for n, (source, target) in enumerate((
            (cells_hbm, cells_ref), (proj_hbm, proj_ref), (x_hbm, x_ref), (p_hbm, p_ref),
            (pot_hbm, pot_ref), (scale_hbm, scale_ref), (prior_hbm, prior_ref)))
    ]
    for copy in loads:
        copy.start()
    lax.fori_loop(1, ndev, greet, 0)
    for copy in loads:
        copy.wait()

    def load(i, carry):
        ext[0, edge + i] = x_ref[pl.ds(i, states, stride=lines), :]
        ext[1, edge + i] = p_ref[pl.ds(i, states, stride=lines), :]
        return carry

    lax.fori_loop(0, lines, load, 0)

    @pl.when(jnp.logical_not(has_prev))
    def _():
        for b in range(3):
            ext[b, 0:edge] = jnp.zeros((edge, states, wz), F32)
            cprev[b] = jnp.zeros_like(cprev[b])
        prev_cells[...] = jnp.zeros_like(prev_cells)
        prev_proj[...] = jnp.zeros_like(prev_proj)

    @pl.when(jnp.logical_not(has_next))
    def _():
        for b in range(3):
            ext[b, edge + lines :] = jnp.zeros((edge, states, wz), F32)

    def dense(cells, proj, first, count, out_h, out_l):
        per = 8 // nproj
        line_iota = lax.broadcasted_iota(jnp.int32, (count, 8, per * wz), 0) + first
        lane_iota = lax.broadcasted_iota(jnp.int32, (wz, per * wz), 0)
        row_iota = lax.broadcasted_iota(jnp.int32, (8, wz), 0)
        for pair in range(slots // per // 2):
            made = ([], [])
            for q in (2 * pair, 2 * pair + 1):
                values = proj[8 * q : 8 * q + 8, :]
                spread = jnp.concatenate(
                    [jnp.where(row_iota // nproj == u, values, 0.0) for u in range(per)], axis=1
                )
                where = jnp.concatenate(
                    [cells[per * q + u : per * q + u + 1, :] for u in range(per)], axis=1
                )
                hot = jnp.where(lane_iota == where % wz, 1.0, 0.0).astype(BF16)
                hit = line_iota == (where // wz)[None]
                for source, out in zip(split(spread), made):
                    left = jnp.where(hit, source.astype(F32)[None], 0.0)
                    left = left.reshape(count * 8, per * wz).astype(BF16)
                    out.append(dot_nt(left, hot).reshape(count, 8, wz))
            for parts, out in zip(made, (out_h, out_l)):
                out[0:count, 16 * pair : 16 * pair + 16, :] = jnp.concatenate(
                    parts, axis=1).astype(BF16)

    dense(cells_ref, proj_ref, 0, lines + edge, dens_h, dens_l)

    pl.semaphore_wait(barrier, ndev - 1)

    def up_copy(b):
        return pltpu.make_async_remote_copy(
            ext.at[b, pl.ds(lines, edge)], ext.at[b, pl.ds(0, edge)],
            halo_send.at[2 * b], halo_recv.at[2 * b], behind, MESH)

    def down_copy(b):
        return pltpu.make_async_remote_copy(
            ext.at[b, pl.ds(edge, edge)], ext.at[b, pl.ds(edge + lines, edge)],
            halo_send.at[2 * b + 1], halo_recv.at[2 * b + 1], before, MESH)

    def meta_copies():
        return (
            pltpu.make_async_remote_copy(
                cells_ref, prev_cells, meta_send.at[0], meta_recv.at[0], behind, MESH),
            pltpu.make_async_remote_copy(
                proj_ref, prev_proj, meta_send.at[1], meta_recv.at[1], behind, MESH),
        )

    def c_copy(b):
        return pltpu.make_async_remote_copy(
            csend.at[b], cprev.at[b], c_send.at[b], c_recv.at[b], behind, MESH)

    def start_halo(b):
        @pl.when(has_next)
        def _():
            up_copy(b).start()

        @pl.when(has_prev)
        def _():
            down_copy(b).start()

    def block_lines(b):
        return (ext.at[b], edge) if b < 3 else (fin.at[b - 3], 0)

    def band_copy(b, d):
        t = lax.rem(band + d, nb)
        ref, base = block_lines(b)
        return pltpu.make_async_remote_copy(
            ref.at[pl.ds(base + part * t, part)],
            s_ref.at[b, :, pl.ds(pl.multiple_of(band * states, states), states), :],
            band_send.at[b, d - 1], band_recv.at[b, d - 1], (t, grid), MESH)

    def start_band(b):
        for d in range(1, nb):
            band_copy(b, d).start()
        ref, base = block_lines(b)
        s_ref[b, :, pl.ds(pl.multiple_of(band * states, states), states), :] = ref[
            pl.ds(base + part * band, part)]

    @pl.when(has_next)
    def _():
        for copy in meta_copies():
            copy.start()

    start_halo(0)
    start_band(0)
    start_halo(1)
    start_band(1)

    @pl.when(has_prev)
    def _():
        for copy in meta_copies():
            copy.wait_recv()

    dense(prev_cells, prev_proj, lines, edge, prev_h, prev_l)

    lane = lax.broadcasted_iota(jnp.int32, (1, wz), 1)
    ups = [jnp.where(lane >= k, HOP[k], 0.0).astype(F32) for k in range(1, 7)]
    downs = [jnp.where(lane < wz - k, HOP[k], 0.0).astype(F32) for k in range(1, 7)]

    def wide(ref, first):
        return jnp.concatenate([ref[first + y] for y in range(wy)], axis=1)

    def apply(b, store):
        @pl.when(has_prev)
        def _():
            up_copy(b).wait_recv()

        @pl.when(has_next)
        def _():
            down_copy(b).wait_recv()

        def project(p, carry):
            value = jnp.concatenate([ext[b, edge + wy * p + y] for y in range(wy)], axis=1)
            high, low = split(value)
            d_h = wide(dens_h, wy * p)
            d_l = wide(dens_l, wy * p)
            both = dot_nt(high, d_h) + dot_nt(low, d_h)
            return carry + both + dot_nt(high, d_l)

        coefficient = lax.fori_loop(
            0, planes + HALO, project, jnp.zeros((states, rows), F32), unroll=2)
        scaled = coefficient * scale_ref[...]
        csend[b, :, 0:rows] = scaled

        @pl.when(has_next)
        def _():
            c_copy(b).start()

        own_h, own_l = split(scaled)

        def plane(p, carry):
            here = edge + wy * p
            center = [ext[b, here + y] for y in range(wy)]
            d_h = wide(dens_h, wy * p)
            d_l = wide(dens_l, wy * p)
            term = dot_nn(own_h, d_h) + dot_nn(own_l, d_h) + dot_nn(own_h, d_l)
            for y in range(wy):
                v = center[y]
                total = pot_ref[pl.ds(wy * p + y, 1), :] * v + term[:, y * wz : (y + 1) * wz]
                for k in range(1, 7):
                    total = total + HOP[k] * (
                        ext[b, here + wy * k + y] + ext[b, here - wy * k + y])
                for other in range(wy):
                    if 0 < abs(other - y) <= 6:
                        total = total + HOP[abs(other - y)] * center[other]
                for k in range(1, 7):
                    total = total + ups[k - 1] * pltpu.roll(v, k, 1)
                    total = total + downs[k - 1] * pltpu.roll(v, wz - k, 1)
                store(wy * p + y, total)
            return carry

        lax.fori_loop(0, planes, plane, 0)

        @pl.when(has_prev)
        def _():
            c_copy(b).wait_recv()

        got_h, got_l = split(cprev[b, :, 0:rows])

        def outer(p, carry):
            d_h = wide(prev_h, wy * p)
            d_l = wide(prev_l, wy * p)
            term = dot_nn(got_h, d_h) + dot_nn(got_l, d_h) + dot_nn(got_h, d_l)
            for y in range(wy):
                store(wy * p + y, term[:, y * wz : (y + 1) * wz], True)
            return carry

        lax.fori_loop(0, HALO, outer, 0)

    def store_to(ref, base):
        def store(i, value, add=False):
            if add:
                ref[base + i] = ref[base + i] + value
            else:
                ref[base + i] = value
        return store

    apply(0, store_to(ext.at[2], edge))
    start_halo(2)
    start_band(2)
    apply(1, store_to(fin.at[0], 0))
    start_band(3)
    apply(2, store_to(fin.at[1], 0))
    start_band(4)

    for b in range(BLOCKS):
        for d in range(1, nb):
            band_copy(b, d).wait_recv()

    many = 4 if part % 4 == 0 else 1

    def gram(i, carry):
        value = jnp.concatenate(
            [
                jnp.concatenate([s_ref[b, many * i + u] for b in range(BLOCKS)], axis=0)
                for u in range(many)
            ],
            axis=1,
        )
        high, low = split(value)
        return carry + dot_nt(high, high) + dot_nt(high, low) + dot_nt(low, high)

    total = lax.fori_loop(
        0, part // many, gram, jnp.zeros((BLOCKS * NB, BLOCKS * NB), F32))
    for n, (i, j) in enumerate(PAIRS):
        gpart[NB * (n // 2) : NB * (n // 2) + NB, NB * (n % 2) : NB * (n % 2) + NB] = total[
            NB * i : NB * i + NB, NB * j : NB * j + NB]
    gpart[NB * 7 :, NB:] = jnp.zeros((NB, NB), F32)

    share = gpart.shape[0] // owners

    def piece(index):
        return pl.ds(pl.multiple_of(index * share, share), share)

    def device(t):
        return (t // ng, lax.rem(t, ng))

    def rs_copy(d):
        t = lax.rem(me + d, ndev)
        return t, pltpu.make_async_remote_copy(
            gpart.at[piece(jnp.minimum(t, owners - 1))], grecv.at[d - 1],
            rs_send.at[d - 1], rs_recv.at[d - 1], device(t), MESH)

    def ag_copy(d, source):
        t = lax.rem(me + d, ndev)
        mine = piece(jnp.minimum(source, owners - 1))
        return pltpu.make_async_remote_copy(
            gown, g_ref.at[mine], ag_send.at[d - 1], ag_recv.at[d - 1], device(t), MESH)

    def guard(cond, body):
        if owners == ndev:
            body()
        else:
            pl.when(cond)(body)

    def rs_start(d, carry):
        t, copy = rs_copy(d)
        guard(t < owners, lambda: copy.start())
        return carry

    lax.fori_loop(1, ndev, rs_start, 0)

    def own_sum():
        def add(d, acc):
            _, copy = rs_copy(d)
            copy.wait_recv()
            return acc + grecv[d - 1]

        summed = lax.fori_loop(1, ndev, add, gpart[piece(jnp.minimum(me, owners - 1)), :])
        gown[...] = summed
        g_ref[piece(jnp.minimum(me, owners - 1)), :] = summed

        def ag_start(d, carry):
            ag_copy(d, me).start()
            return carry

        lax.fori_loop(1, ndev, ag_start, 0)

    guard(me < owners, own_sum)

    def ag_wait(d, carry):
        source = lax.rem(me + ndev - d, ndev)
        guard(source < owners, lambda: ag_copy(d, source).wait_recv())
        return carry

    lax.fori_loop(1, ndev, ag_wait, 0)

    inverse_total = 1.0 / (lines * ng * wz)
    for n, (i, j) in enumerate(PAIRS):
        block = g_ref[NB * (n // 2) : NB * (n // 2) + NB, NB * (n % 2) : NB * (n % 2) + NB]
        block = block * inverse_total
        whole[NB * i : NB * i + NB, NB * j : NB * j + NB] = block
        if i != j:
            whole[NB * j : NB * j + NB, NB * i : NB * i + NB] = block.T

    def full_nn(a, b):
        return lax.dot_general(
            a, b, (((1,), (0,)), ((), ())), precision=HIGHEST, preferred_element_type=F32)

    def full_nt(a, b):
        return lax.dot_general(
            a, b, (((1,), (1,)), ((), ())), precision=HIGHEST, preferred_element_type=F32)

    row = lax.broadcasted_iota(jnp.int32, (NB, NB), 0)
    col = lax.broadcasted_iota(jnp.int32, (NB, NB), 1)
    identity = jnp.where(row == col, 1.0, 0.0).astype(F32)

    def factor(gram_matrix):
        mat[:, 0:NB] = gram_matrix
        mat[:, NB:] = identity
        factor_in_place(mat)
        return jnp.where(col >= row, mat[:, 0:NB], 0.0), mat[:, NB:]

    _, inverse0 = factor(whole[0:NB, 0:NB])
    half = full_nn(inverse0, whole[0:NB, 2 * NB : 3 * NB])
    a0 = full_nt(half, inverse0)
    co[:, 0:NB] = -full_nn(full_nt(inverse0, half), inverse0)
    co[:, NB : 2 * NB] = -prior_ref[...]
    co[:, 2 * NB : 3 * NB] = inverse0
    w0 = co[:, 0 : 3 * NB]
    upper1, inverse1 = factor(full_nt(full_nn(w0, whole[0 : 3 * NB, 0 : 3 * NB]), w0))
    q1 = full_nn(inverse1, w0)
    half = full_nn(q1, whole[0 : 3 * NB, 2 * NB : 5 * NB])
    a1 = full_nt(half, q1)
    past = full_nn(full_nt(q1, half), q1)
    co[:, 2 * NB : 5 * NB] = q1
    co[:, 0:NB] = -past[:, 0:NB] - full_nn(upper1, inverse0)
    co[:, NB : 2 * NB] = -past[:, NB : 2 * NB]
    co[:, 2 * NB : 3 * NB] = co[:, 2 * NB : 3 * NB] - past[:, 2 * NB : 3 * NB]
    w1 = co[...]
    upper2, inverse2 = factor(full_nt(full_nn(w1, whole[...]), w1))
    q2 = full_nn(inverse2, w1)

    c_high, c_low = split(q2)
    many = 2 if part % 2 == 0 else 1

    def combine(i, carry):
        value = jnp.concatenate(
            [
                jnp.concatenate([s_ref[b, many * i + u] for b in range(BLOCKS)], axis=0)
                for u in range(many)
            ],
            axis=1,
        )
        v_h, v_l = split(value)
        made = dot_nn(c_high, v_h) + dot_nn(c_low, v_h) + dot_nn(c_high, v_l)
        for t in range(nb):
            for u in range(many):
                mine[t, many * i + u] = made[
                    t * states : (t + 1) * states, u * wz : (u + 1) * wz]
        return carry

    lax.fori_loop(0, part // many, combine, 0, unroll=2 if part // many > 1 else 1)

    def out_copy(d):
        t = lax.rem(band + d, nb)
        return pltpu.make_async_remote_copy(
            mine.at[t], got.at[band], out_send.at[d - 1], out_recv.at[d - 1], (t, grid), MESH)

    for d in range(1, nb):
        out_copy(d).start()

    def put(source, ref):
        def line(i, carry):
            q_ref[pl.ds(source * part + i, states, stride=lines), :] = ref[i]
            return carry

        lax.fori_loop(0, part, line, 0)

    put(band, mine.at[band])
    pick = jnp.where(
        lax.broadcasted_iota(jnp.int32, (NB, states), 0)
        == lax.broadcasted_iota(jnp.int32, (NB, states), 1) + band * states, 1.0, 0.0).astype(F32)
    outs = (a0 + SHIFT * identity, a1 + SHIFT * identity, upper1, upper2)
    for n, value in enumerate(outs):
        small_ref[n] = full_nn(value, pick)

    def drain(d, carry):
        t, copy = rs_copy(d)
        guard(t < owners, lambda: copy.wait_send())
        guard(me < owners, lambda: ag_copy(d, me).wait_send())
        return carry

    lax.fori_loop(1, ndev, drain, 0)

    for b in range(BLOCKS):
        for d in range(1, nb):
            band_copy(b, d).wait_send()

    @pl.when(has_next)
    def _():
        for b in range(3):
            up_copy(b).wait_send()
            c_copy(b).wait_send()
        for copy in meta_copies():
            copy.wait_send()

    @pl.when(has_prev)
    def _():
        for b in range(3):
            down_copy(b).wait_send()

    for d in range(1, nb):
        out_copy(d).wait_recv()
        source = lax.rem(band + nb - d, nb)
        put(source, got.at[source])
    for d in range(1, nb):
        out_copy(d).wait_send()


def factor_in_place(mat):
    tall, width = mat.shape
    tiles = [mat[8 * i : 8 * i + 8, :] for i in range(tall // 8)]
    sublane = lax.broadcasted_iota(jnp.int32, (8, width), 0)
    for j in range(tall // 8):
        columns = [
            {
                i: jnp.broadcast_to(tiles[i][:, 8 * j + c : 8 * j + c + 1], (8, width))
                for i in range(j, tall // 8)
            }
            for c in range(8)
        ]
        roots = jnp.ones((8, width), F32)
        for c in range(8):
            pivot = jnp.broadcast_to(columns[c][j][c : c + 1, :], (8, width))
            line = jnp.broadcast_to(tiles[j][c : c + 1, :], (8, width))
            roots = jnp.where(sublane == c, pivot, roots)
            inverse = 1.0 / pivot
            tops = {k: jnp.broadcast_to(columns[k][j][c : c + 1, :], (8, width)) for k in range(c + 1, 8)}
            for i in range(j, tall // 8):
                ratio = columns[c][i] * inverse
                if i == j:
                    ratio = jnp.where(sublane > c, ratio, 0.0)
                tiles[i] = tiles[i] - ratio * line
                for k in range(c + 1, 8):
                    columns[k][i] = columns[k][i] - ratio * tops[k]
        mat[8 * j : 8 * j + 8, :] = tiles[j] / jnp.sqrt(roots)


def shards(
    start_block,
    previous_block,
    previous_coupling,
    potential,
    atom_cells,
    atom_proj,
    atom_strength,
    atom_count,
):
    states, planes, wy, wz = start_block.shape
    slots, nproj, points = atom_proj.shape
    nb, ng = lax.axis_size("band"), lax.axis_size("grid")
    ndev = nb * ng
    lines = planes * wy
    edge = HALO * wy
    part = lines // nb
    rows = slots * nproj
    owners = min(ndev, 64)
    live = (jnp.arange(slots, dtype=jnp.int32) < atom_count[0]).astype(F32)
    scale = (atom_strength * live[:, None]).reshape(1, rows)
    dma = pltpu.SemaphoreType.DMA
    vmem = pl.BlockSpec(memory_space=pltpu.VMEM)
    grows = NB * 8
    share = grows // owners
    small, final = pl.pallas_call(
        functools.partial(krylov_kernel, nb, ng, planes, wy, slots, nproj, owners),
        out_shape=(
            jax.ShapeDtypeStruct((2 * STEPS, NB, states), F32),
            jax.ShapeDtypeStruct((states * lines, wz), F32),
        ),
        in_specs=[pl.BlockSpec(memory_space=pl.ANY)] * 7,
        out_specs=(vmem, vmem),
        scratch_shapes=[
            pltpu.VMEM((states * lines, wz), F32),
            pltpu.VMEM((states * lines, wz), F32),
            pltpu.VMEM((lines, wz), F32),
            pltpu.VMEM((slots, points), jnp.int32),
            pltpu.VMEM((rows, points), F32),
            pltpu.VMEM((1, rows), F32),
            pltpu.VMEM((NB, NB), F32),
            dma((7,)),
            pltpu.VMEM((BLOCKS, part, NB, wz), F32),
            pltpu.VMEM((grows, 2 * NB), F32),
            pltpu.VMEM((BLOCKS * NB, BLOCKS * NB), F32),
            pltpu.VMEM((NB, BLOCKS * NB), F32),
            pltpu.VMEM((NB, 2 * NB), F32),
            pltpu.VMEM((nb, part, states, wz), F32),
            pltpu.VMEM((nb, part, states, wz), F32),
            dma((nb - 1,)), dma((nb - 1,)),
            pltpu.VMEM((3, lines + 2 * edge, states, wz), F32),
            pltpu.VMEM((2, lines, states, wz), F32),
            pltpu.VMEM((lines + edge, rows, wz), BF16),
            pltpu.VMEM((lines + edge, rows, wz), BF16),
            pltpu.VMEM((edge, rows, wz), BF16),
            pltpu.VMEM((edge, rows, wz), BF16),
            pltpu.VMEM((slots, points), jnp.int32),
            pltpu.VMEM((rows, points), F32),
            pltpu.VMEM((3, states, 128), F32),
            pltpu.VMEM((3, states, 128), F32),
            pltpu.VMEM((grows, 2 * NB), F32),
            pltpu.VMEM((ndev - 1, share, 2 * NB), F32),
            pltpu.VMEM((share, 2 * NB), F32),
            dma((6,)), dma((6,)), dma((2,)), dma((2,)), dma((3,)), dma((3,)),
            dma((BLOCKS, nb - 1)), dma((BLOCKS, nb - 1)),
            dma((ndev - 1,)), dma((ndev - 1,)), dma((ndev - 1,)), dma((ndev - 1,)),
        ],
        compiler_params=pltpu.CompilerParams(
            collective_id=0, has_side_effects=True, vmem_limit_bytes=60 * 2**20),
    )(
        start_block.reshape(states * lines, wz),
        previous_block.reshape(states * lines, wz),
        potential.reshape(lines, wz),
        atom_cells,
        atom_proj.reshape(rows, points),
        scale,
        previous_coupling,
    )
    return (small[:STEPS], small[STEPS:], final.reshape(start_block.shape))


def solution(mesh):
    in_specs = (
        P("band", "grid", None, None),
        P("band", "grid", None, None),
        P(),
        P("grid", None, None),
        P("grid", None),
        P("grid", None, None),
        P("grid", None),
        P("grid"),
    )
    out_specs = (P(None, None, "band"), P(None, None, "band"), P("band", "grid", None, None))
    return jax.shard_map(shards, mesh=mesh, in_specs=in_specs, out_specs=out_specs, check_vma=False)
```

```python
import functools

import jax
import jax.numpy as jnp
from jax import lax
from jax.experimental import pallas as pl
from jax.experimental.pallas import tpu as pltpu
from jax.sharding import PartitionSpec as P

NB = 64
STEPS = 2
HALO = 6
MESH = pl.DeviceIdType.MESH

HIGHEST = lax.Precision.HIGHEST
STENCIL_WEIGHTS = (
    -5369.0 / 1800.0,
    12.0 / 7.0,
    -15.0 / 56.0,
    10.0 / 189.0,
    -1.0 / 112.0,
    2.0 / 1925.0,
    -1.0 / 16632.0,
)
HOP = tuple(-0.5 * w for w in STENCIL_WEIGHTS)
SHIFT = 3.0 * HOP[0]
BLOCKS = 5
FIRST = ((0, 0), (0, 1), (0, 2), (0, 3), (1, 1), (1, 2), (1, 3), (2, 2), (2, 3), (3, 3))
SECOND = ((1, 4), (2, 4), (3, 4), (4, 4))
BASES = (0, 320)
SHARES = (16, 8)
OWNERS = (20, 16)
F32 = jnp.float32
BF16 = jnp.bfloat16


def split(x):
    high = x.astype(BF16)
    return high, (x - high.astype(F32)).astype(BF16)


def dot_nt(a, b):
    return lax.dot_general(a, b, (((1,), (1,)), ((), ())), preferred_element_type=F32)


def dot_nn(a, b):
    return lax.dot_general(a, b, (((1,), (0,)), ((), ())), preferred_element_type=F32)


def krylov_kernel(
    nb, ng, planes, wy, slots, nproj,
    x_hbm, p_hbm, pot_hbm, cells_hbm, proj_hbm, scale_hbm, prior_hbm,
    a_ref, b_ref, q_ref,
    x_ref, p_ref, pot_ref, cells_ref, proj_ref, scale_ref, prior_ref, in_sems,
    s_ref, g_ref, whole, co, mat, mine, got, out_send, out_recv,
    ext, fin, dens_h, dens_l, prev_h, prev_l, prev_cells, prev_proj,
    csend, cprev, gpart, grecv_a, grecv_b, gown_a, gown_b,
    halo_send, halo_recv, meta_send, meta_recv, c_send, c_recv,
    band_send, band_recv, rs_send, rs_recv, ag_send, ag_recv,
):
    ndev = nb * ng
    states = x_ref.shape[0] // (planes * wy)
    lines = planes * wy
    edge = HALO * wy
    part = lines // nb
    rows = slots * nproj
    wz = x_ref.shape[1]
    span = wy * wz
    band = lax.axis_index("band")
    grid = lax.axis_index("grid")
    me = band * ng + grid
    has_prev = grid > 0
    has_next = grid < ng - 1
    before = (band, jnp.maximum(grid - 1, 0))
    behind = (band, jnp.minimum(grid + 1, ng - 1))

    barrier = pltpu.get_barrier_semaphore()

    def greet(d, carry):
        t = lax.rem(me + d, ndev)
        pl.semaphore_signal(barrier, inc=1, device_id=(t // ng, lax.rem(t, ng)), device_id_type=MESH)
        return carry

    loads = [
        pltpu.make_async_copy(source, target, in_sems.at[n])
        for n, (source, target) in enumerate((
            (cells_hbm, cells_ref), (proj_hbm, proj_ref), (x_hbm, x_ref), (p_hbm, p_ref),
            (pot_hbm, pot_ref), (scale_hbm, scale_ref), (prior_hbm, prior_ref)))
    ]
    for copy in loads:
        copy.start()
    lax.fori_loop(1, ndev, greet, 0)
    for copy in loads:
        copy.wait()

    def load(i, carry):
        ext[0, edge + i] = x_ref[pl.ds(i, states, stride=lines), :]
        ext[1, edge + i] = p_ref[pl.ds(i, states, stride=lines), :]
        return carry

    lax.fori_loop(0, lines, load, 0)

    @pl.when(jnp.logical_not(has_prev))
    def _():
        for b in range(3):
            ext[b, 0:edge] = jnp.zeros((edge, states, wz), F32)
            cprev[b] = jnp.zeros_like(cprev[b])
        prev_cells[...] = jnp.zeros_like(prev_cells)
        prev_proj[...] = jnp.zeros_like(prev_proj)

    @pl.when(jnp.logical_not(has_next))
    def _():
        for b in range(3):
            ext[b, edge + lines :] = jnp.zeros((edge, states, wz), F32)

    def dense(cells, proj, first, count, out_h, out_l):
        per = 8 // nproj
        line_iota = lax.broadcasted_iota(jnp.int32, (count, 8, per * wz), 0) + first
        lane_iota = lax.broadcasted_iota(jnp.int32, (wz, per * wz), 0)
        row_iota = lax.broadcasted_iota(jnp.int32, (8, wz), 0)
        for pair in range(slots // per // 2):
            made = ([], [])
            for q in (2 * pair, 2 * pair + 1):
                values = proj[8 * q : 8 * q + 8, :]
                spread = jnp.concatenate(
                    [jnp.where(row_iota // nproj == u, values, 0.0) for u in range(per)], axis=1
                )
                where = jnp.concatenate(
                    [cells[per * q + u : per * q + u + 1, :] for u in range(per)], axis=1
                )
                hot = jnp.where(lane_iota == where % wz, 1.0, 0.0).astype(BF16)
                hit = line_iota == (where // wz)[None]
                for source, out in zip(split(spread), made):
                    left = jnp.where(hit, source.astype(F32)[None], 0.0)
                    left = left.reshape(count * 8, per * wz).astype(BF16)
                    out.append(dot_nt(left, hot).reshape(count, 8, wz))
            for parts, out in zip(made, (out_h, out_l)):
                out[0:count, 16 * pair : 16 * pair + 16, :] = jnp.concatenate(
                    parts, axis=1).astype(BF16)

    dense(cells_ref, proj_ref, 0, lines + edge, dens_h, dens_l)

    pl.semaphore_wait(barrier, ndev - 1)

    def up_copy(b):
        return pltpu.make_async_remote_copy(
            ext.at[b, pl.ds(lines, edge)], ext.at[b, pl.ds(0, edge)],
            halo_send.at[2 * b], halo_recv.at[2 * b], behind, MESH)

    def down_copy(b):
        return pltpu.make_async_remote_copy(
            ext.at[b, pl.ds(edge, edge)], ext.at[b, pl.ds(edge + lines, edge)],
            halo_send.at[2 * b + 1], halo_recv.at[2 * b + 1], before, MESH)

    def meta_copies():
        return (
            pltpu.make_async_remote_copy(
                cells_ref, prev_cells, meta_send.at[0], meta_recv.at[0], behind, MESH),
            pltpu.make_async_remote_copy(
                proj_ref, prev_proj, meta_send.at[1], meta_recv.at[1], behind, MESH),
        )

    def c_copy(b):
        return pltpu.make_async_remote_copy(
            csend.at[b], cprev.at[b], c_send.at[b], c_recv.at[b], behind, MESH)

    def start_halo(b):
        @pl.when(has_next)
        def _():
            up_copy(b).start()

        @pl.when(has_prev)
        def _():
            down_copy(b).start()

    def block_lines(b):
        return (ext.at[b], edge) if b < 3 else (fin.at[b - 3], 0)

    def band_copy(b, d):
        t = lax.rem(band + d, nb)
        ref, base = block_lines(b)
        return pltpu.make_async_remote_copy(
            ref.at[pl.ds(base + part * t, part)],
            s_ref.at[b, :, pl.ds(pl.multiple_of(band * states, states), states), :],
            band_send.at[b, d - 1], band_recv.at[b, d - 1], (t, grid), MESH)

    def start_band(b):
        for d in range(1, nb):
            band_copy(b, d).start()
        ref, base = block_lines(b)
        s_ref[b, :, pl.ds(pl.multiple_of(band * states, states), states), :] = ref[
            pl.ds(base + part * band, part)]

    @pl.when(has_next)
    def _():
        for copy in meta_copies():
            copy.start()

    start_halo(0)
    start_band(0)
    start_halo(1)
    start_band(1)

    @pl.when(has_prev)
    def _():
        for copy in meta_copies():
            copy.wait_recv()

    dense(prev_cells, prev_proj, lines, edge, prev_h, prev_l)

    lane = lax.broadcasted_iota(jnp.int32, (1, wz), 1)
    ups = [jnp.where(lane >= k, HOP[k], 0.0).astype(F32) for k in range(1, 7)]
    downs = [jnp.where(lane < wz - k, HOP[k], 0.0).astype(F32) for k in range(1, 7)]

    def wide(ref, first):
        return jnp.concatenate([ref[first + y] for y in range(wy)], axis=1)

    def apply(b, store):
        @pl.when(has_prev)
        def _():
            up_copy(b).wait_recv()

        @pl.when(has_next)
        def _():
            down_copy(b).wait_recv()

        def project(p, carry):
            value = jnp.concatenate([ext[b, edge + wy * p + y] for y in range(wy)], axis=1)
            high, low = split(value)
            d_h = wide(dens_h, wy * p)
            d_l = wide(dens_l, wy * p)
            both = dot_nt(high, d_h) + dot_nt(low, d_h)
            return carry + both + dot_nt(high, d_l)

        coefficient = lax.fori_loop(
            0, planes + HALO, project, jnp.zeros((states, rows), F32), unroll=2)
        scaled = coefficient * scale_ref[...]
        csend[b, :, 0:rows] = scaled

        @pl.when(has_next)
        def _():
            c_copy(b).start()

        own_h, own_l = split(scaled)

        def plane(p, carry):
            here = edge + wy * p
            center = [ext[b, here + y] for y in range(wy)]
            d_h = wide(dens_h, wy * p)
            d_l = wide(dens_l, wy * p)
            term = dot_nn(own_h, d_h) + dot_nn(own_l, d_h) + dot_nn(own_h, d_l)
            for y in range(wy):
                v = center[y]
                total = pot_ref[pl.ds(wy * p + y, 1), :] * v + term[:, y * wz : (y + 1) * wz]
                for k in range(1, 7):
                    total = total + HOP[k] * (
                        ext[b, here + wy * k + y] + ext[b, here - wy * k + y])
                for other in range(wy):
                    if 0 < abs(other - y) <= 6:
                        total = total + HOP[abs(other - y)] * center[other]
                for k in range(1, 7):
                    total = total + ups[k - 1] * pltpu.roll(v, k, 1)
                    total = total + downs[k - 1] * pltpu.roll(v, wz - k, 1)
                store(wy * p + y, total)
            return carry

        lax.fori_loop(0, planes, plane, 0)

        @pl.when(has_prev)
        def _():
            c_copy(b).wait_recv()

        got_h, got_l = split(cprev[b, :, 0:rows])

        def outer(p, carry):
            d_h = wide(prev_h, wy * p)
            d_l = wide(prev_l, wy * p)
            term = dot_nn(got_h, d_h) + dot_nn(got_l, d_h) + dot_nn(got_h, d_l)
            for y in range(wy):
                store(wy * p + y, term[:, y * wz : (y + 1) * wz], True)
            return carry

        lax.fori_loop(0, HALO, outer, 0)

    def store_to(ref, base):
        def store(i, value, add=False):
            if add:
                ref[base + i] = ref[base + i] + value
            else:
                ref[base + i] = value
        return store

    apply(0, store_to(ext.at[2], edge))
    start_halo(2)
    start_band(2)
    apply(1, store_to(fin.at[0], 0))
    start_band(3)
    apply(2, store_to(fin.at[1], 0))
    start_band(4)

    grecv, gown = (grecv_a, grecv_b), (gown_a, gown_b)

    def piece(s, t):
        index = (OWNERS[s] * t) // ndev
        return pl.ds(pl.multiple_of(BASES[s] + index * SHARES[s], 8), SHARES[s])

    def slot(s, t):
        return s * OWNERS[0] + (OWNERS[s] * t) // ndev

    def owner(s, t):
        return lax.rem(OWNERS[s] * t, ndev) < OWNERS[s]

    def device(t):
        return (t // ng, lax.rem(t, ng))

    def rs_copy(s, d):
        t = lax.rem(me + d, ndev)
        return t, pltpu.make_async_remote_copy(
            gpart.at[piece(s, t)], grecv[s].at[d - 1],
            rs_send.at[slot(s, t)], rs_recv.at[s, d - 1], device(t), MESH)

    def ag_copy(s, d, source):
        t = lax.rem(me + d, ndev)
        return pltpu.make_async_remote_copy(
            gown[s], g_ref.at[piece(s, source)],
            ag_send.at[s, d - 1], ag_recv.at[slot(s, source)], device(t), MESH)

    def scatter(s):
        def start(d, carry):
            t, copy = rs_copy(s, d)

            @pl.when(owner(s, t))
            def _():
                copy.start()

            return carry

        lax.fori_loop(1, ndev, start, 0)

    def add_up(s):
        @pl.when(owner(s, me))
        def _():
            def add(d, acc):
                rs_copy(s, d)[1].wait_recv()
                return acc + grecv[s][d - 1]

            summed = lax.fori_loop(1, ndev, add, gpart[piece(s, me), :])
            gown[s][...] = summed
            g_ref[piece(s, me), :] = summed

            def start(d, carry):
                ag_copy(s, d, me).start()
                return carry

            lax.fori_loop(1, ndev, start, 0)

    def collect(s, pairs):
        def arrive(d, carry):
            source = lax.rem(me + ndev - d, ndev)

            @pl.when(owner(s, source))
            def _():
                ag_copy(s, d, source).wait_recv()

            return carry

        lax.fori_loop(1, ndev, arrive, 0)
        inverse_total = 1.0 / (lines * ng * wz)
        for n, (i, j) in enumerate(pairs):
            top, side = BASES[s] + NB * (n // 2), NB * (n % 2)
            block = g_ref[top : top + NB, side : side + NB] * inverse_total
            whole[NB * i : NB * i + NB, NB * j : NB * j + NB] = block
            if i != j:
                whole[NB * j : NB * j + NB, NB * i : NB * i + NB] = block.T

    many = 4 if part % 4 == 0 else 1

    def stacked(i, first):
        return jnp.concatenate(
            [
                jnp.concatenate([s_ref[b, many * i + u] for b in range(first, first + 4)], axis=0)
                for u in range(many)
            ],
            axis=1,
        )

    def gram_first(i, carry):
        high, low = split(stacked(i, 0))
        return carry + dot_nt(high, high) + dot_nt(high, low) + dot_nt(low, high)

    def gram_second(i, carry):
        high, low = split(stacked(i, 1))
        return (
            carry + dot_nt(high, high[3 * NB :]) + dot_nt(high, low[3 * NB :])
            + dot_nt(low, high[3 * NB :]))

    for b in range(BLOCKS - 1):
        for d in range(1, nb):
            band_copy(b, d).wait_recv()
    total = lax.fori_loop(0, part // many, gram_first, jnp.zeros((4 * NB, 4 * NB), F32))
    for n, (i, j) in enumerate(FIRST):
        top, side = NB * (n // 2), NB * (n % 2)
        gpart[top : top + NB, side : side + NB] = total[NB * i : NB * i + NB, NB * j : NB * j + NB]
    scatter(0)
    for d in range(1, nb):
        band_copy(BLOCKS - 1, d).wait_recv()
    total = lax.fori_loop(0, part // many, gram_second, jnp.zeros((4 * NB, NB), F32))
    for n in range(4):
        top, side = BASES[1] + NB * (n // 2), NB * (n % 2)
        gpart[top : top + NB, side : side + NB] = total[NB * n : NB * n + NB, :]
    scatter(1)
    add_up(0)
    add_up(1)
    collect(0, FIRST)

    def full_nn(a, b):
        return lax.dot_general(
            a, b, (((1,), (0,)), ((), ())), precision=HIGHEST, preferred_element_type=F32)

    def full_nt(a, b):
        return lax.dot_general(
            a, b, (((1,), (1,)), ((), ())), precision=HIGHEST, preferred_element_type=F32)

    row = lax.broadcasted_iota(jnp.int32, (NB, NB), 0)
    col = lax.broadcasted_iota(jnp.int32, (NB, NB), 1)
    identity = jnp.where(row == col, 1.0, 0.0).astype(F32)

    def factor(gram_matrix):
        mat[:, 0:NB] = gram_matrix
        mat[:, NB:] = identity
        factor_in_place(mat)
        return jnp.where(col >= row, mat[:, 0:NB], 0.0), mat[:, NB:]

    _, inverse0 = factor(whole[0:NB, 0:NB])
    half = full_nn(inverse0, whole[0:NB, 2 * NB : 3 * NB])
    a0 = full_nt(half, inverse0)
    co[:, 0:NB] = -full_nn(full_nt(inverse0, half), inverse0)
    co[:, NB : 2 * NB] = -prior_ref[...]
    co[:, 2 * NB : 3 * NB] = inverse0
    w0 = co[:, 0 : 3 * NB]
    upper1, inverse1 = factor(full_nt(full_nn(w0, whole[0 : 3 * NB, 0 : 3 * NB]), w0))
    q1 = full_nn(inverse1, w0)
    collect(1, SECOND)
    corner = whole[2 * NB : 3 * NB, 2 * NB : 3 * NB]
    whole[0:NB, 4 * NB :] = corner
    whole[4 * NB :, 0:NB] = corner
    half = full_nn(q1, whole[0 : 3 * NB, 2 * NB : 5 * NB])
    a1 = full_nt(half, q1)
    past = full_nn(full_nt(q1, half), q1)
    co[:, 2 * NB : 5 * NB] = q1
    co[:, 0:NB] = -past[:, 0:NB] - full_nn(upper1, inverse0)
    co[:, NB : 2 * NB] = -past[:, NB : 2 * NB]
    co[:, 2 * NB : 3 * NB] = co[:, 2 * NB : 3 * NB] - past[:, 2 * NB : 3 * NB]
    w1 = co[...]
    upper2, inverse2 = factor(full_nt(full_nn(w1, whole[...]), w1))
    q2 = full_nn(inverse2, w1)

    c_high, c_low = split(q2)
    pair = 2 if part % 2 == 0 else 1

    def combine(i, carry):
        value = jnp.concatenate(
            [
                jnp.concatenate([s_ref[b, pair * i + u] for b in range(BLOCKS)], axis=0)
                for u in range(pair)
            ],
            axis=1,
        )
        v_h, v_l = split(value)
        made = dot_nn(c_high, v_h) + dot_nn(c_low, v_h) + dot_nn(c_high, v_l)
        for t in range(nb):
            for u in range(pair):
                mine[t, pair * i + u] = made[
                    t * states : (t + 1) * states, u * wz : (u + 1) * wz]
        return carry

    lax.fori_loop(0, part // pair, combine, 0, unroll=2 if part // pair > 1 else 1)

    def out_copy(d):
        t = lax.rem(band + d, nb)
        return pltpu.make_async_remote_copy(
            mine.at[t], got.at[band], out_send.at[d - 1], out_recv.at[d - 1], (t, grid), MESH)

    for d in range(1, nb):
        out_copy(d).start()

    def put(source, ref):
        def line(i, carry):
            q_ref[pl.ds(source * part + i, states, stride=lines), :] = ref[i]
            return carry

        lax.fori_loop(0, part, line, 0)

    put(band, mine.at[band])
    pick = jnp.where(
        lax.broadcasted_iota(jnp.int32, (states, NB), 1)
        == lax.broadcasted_iota(jnp.int32, (states, NB), 0) + band * states, 1.0, 0.0).astype(F32)
    outs = (a0 + SHIFT * identity, a1 + SHIFT * identity, upper1, upper2)
    for n, value in enumerate(outs):
        small = (a_ref, b_ref)[n // STEPS]
        small[n % STEPS] = full_nt(pick, value)

    def drain(d, carry):
        for s in range(2):
            t, copy = rs_copy(s, d)

            @pl.when(owner(s, t))
            def _():
                copy.wait_send()

            @pl.when(owner(s, me))
            def _():
                ag_copy(s, d, me).wait_send()

        return carry

    lax.fori_loop(1, ndev, drain, 0)

    for b in range(BLOCKS):
        for d in range(1, nb):
            band_copy(b, d).wait_send()

    @pl.when(has_next)
    def _():
        for b in range(3):
            up_copy(b).wait_send()
            c_copy(b).wait_send()
        for copy in meta_copies():
            copy.wait_send()

    @pl.when(has_prev)
    def _():
        for b in range(3):
            down_copy(b).wait_send()

    for d in range(1, nb):
        out_copy(d).wait_recv()
        source = lax.rem(band + nb - d, nb)
        put(source, got.at[source])
    for d in range(1, nb):
        out_copy(d).wait_send()


def factor_in_place(mat):
    tall, width = mat.shape
    tiles = [mat[8 * i : 8 * i + 8, :] for i in range(tall // 8)]
    sublane = lax.broadcasted_iota(jnp.int32, (8, width), 0)
    for j in range(tall // 8):
        columns = [
            {
                i: jnp.broadcast_to(tiles[i][:, 8 * j + c : 8 * j + c + 1], (8, width))
                for i in range(j, tall // 8)
            }
            for c in range(8)
        ]
        roots = jnp.ones((8, width), F32)
        for c in range(8):
            pivot = jnp.broadcast_to(columns[c][j][c : c + 1, :], (8, width))
            line = jnp.broadcast_to(tiles[j][c : c + 1, :], (8, width))
            roots = jnp.where(sublane == c, pivot, roots)
            inverse = 1.0 / pivot
            tops = {k: jnp.broadcast_to(columns[k][j][c : c + 1, :], (8, width)) for k in range(c + 1, 8)}
            for i in range(j, tall // 8):
                ratio = columns[c][i] * inverse
                if i == j:
                    ratio = jnp.where(sublane > c, ratio, 0.0)
                tiles[i] = tiles[i] - ratio * line
                for k in range(c + 1, 8):
                    columns[k][i] = columns[k][i] - ratio * tops[k]
        mat[8 * j : 8 * j + 8, :] = tiles[j] / jnp.sqrt(roots)


def shards(
    start_block,
    previous_block,
    previous_coupling,
    potential,
    atom_cells,
    atom_proj,
    atom_strength,
    atom_count,
):
    states, planes, wy, wz = start_block.shape
    slots, nproj, points = atom_proj.shape
    nb, ng = lax.axis_size("band"), lax.axis_size("grid")
    ndev = nb * ng
    lines = planes * wy
    edge = HALO * wy
    part = lines // nb
    rows = slots * nproj
    live = (jnp.arange(slots, dtype=jnp.int32) < atom_count[0]).astype(F32)
    scale = (atom_strength * live[:, None]).reshape(1, rows)
    dma = pltpu.SemaphoreType.DMA
    vmem = pl.BlockSpec(memory_space=pltpu.VMEM)
    grows = NB * 7
    a_rows, b_rows, final = pl.pallas_call(
        functools.partial(krylov_kernel, nb, ng, planes, wy, slots, nproj),
        out_shape=(
            jax.ShapeDtypeStruct((STEPS, states, NB), F32),
            jax.ShapeDtypeStruct((STEPS, states, NB), F32),
            jax.ShapeDtypeStruct((states * lines, wz), F32),
        ),
        in_specs=[pl.BlockSpec(memory_space=pl.ANY)] * 7,
        out_specs=(vmem, vmem, vmem),
        scratch_shapes=[
            pltpu.VMEM((states * lines, wz), F32),
            pltpu.VMEM((states * lines, wz), F32),
            pltpu.VMEM((lines, wz), F32),
            pltpu.VMEM((slots, points), jnp.int32),
            pltpu.VMEM((rows, points), F32),
            pltpu.VMEM((1, rows), F32),
            pltpu.VMEM((NB, NB), F32),
            dma((7,)),
            pltpu.VMEM((BLOCKS, part, NB, wz), F32),
            pltpu.VMEM((grows, 2 * NB), F32),
            pltpu.VMEM((BLOCKS * NB, BLOCKS * NB), F32),
            pltpu.VMEM((NB, BLOCKS * NB), F32),
            pltpu.VMEM((NB, 2 * NB), F32),
            pltpu.VMEM((nb, part, states, wz), F32),
            pltpu.VMEM((nb, part, states, wz), F32),
            dma((nb - 1,)), dma((nb - 1,)),
            pltpu.VMEM((3, lines + 2 * edge, states, wz), F32),
            pltpu.VMEM((2, lines, states, wz), F32),
            pltpu.VMEM((lines + edge, rows, wz), BF16),
            pltpu.VMEM((lines + edge, rows, wz), BF16),
            pltpu.VMEM((edge, rows, wz), BF16),
            pltpu.VMEM((edge, rows, wz), BF16),
            pltpu.VMEM((slots, points), jnp.int32),
            pltpu.VMEM((rows, points), F32),
            pltpu.VMEM((3, states, 128), F32),
            pltpu.VMEM((3, states, 128), F32),
            pltpu.VMEM((grows, 2 * NB), F32),
            pltpu.VMEM((ndev - 1, SHARES[0], 2 * NB), F32),
            pltpu.VMEM((ndev - 1, SHARES[1], 2 * NB), F32),
            pltpu.VMEM((SHARES[0], 2 * NB), F32),
            pltpu.VMEM((SHARES[1], 2 * NB), F32),
            dma((6,)), dma((6,)), dma((2,)), dma((2,)), dma((3,)), dma((3,)),
            dma((BLOCKS, nb - 1)), dma((BLOCKS, nb - 1)),
            dma((sum(OWNERS),)), dma((2, ndev - 1)), dma((2, ndev - 1)), dma((sum(OWNERS),)),
        ],
        compiler_params=pltpu.CompilerParams(
            collective_id=0, has_side_effects=True, vmem_limit_bytes=60 * 2**20),
    )(
        start_block.reshape(states * lines, wz),
        previous_block.reshape(states * lines, wz),
        potential.reshape(lines, wz),
        atom_cells,
        atom_proj.reshape(rows, points),
        scale,
        previous_coupling,
    )
    return (a_rows.swapaxes(1, 2), b_rows.swapaxes(1, 2), final.reshape(start_block.shape))


def solution(mesh):
    in_specs = (
        P("band", "grid", None, None),
        P("band", "grid", None, None),
        P(),
        P("grid", None, None),
        P("grid", None),
        P("grid", None, None),
        P("grid", None),
        P("grid"),
    )
    out_specs = (P(None, None, "band"), P(None, None, "band"), P("band", "grid", None, None))
    return jax.shard_map(shards, mesh=mesh, in_specs=in_specs, out_specs=out_specs, check_vma=False)
```
